32 devices in a mesh: dp: 4 (over y, x), seq: 8 (over z, core).
Axes of the slice: x: 2, y: 2, z: 4, core: 2. Of those that a mesh axis runs over, the one named last changes fastest.
Arguments:
- hidden: bfloat16 [24, 1024, 768], P('dp', 'seq'), may hold values from -6 to 6
- lengths: int32 [24], P('dp'), may hold values from 40 to 1024, as said below
- cotangent: bfloat16 [24, 1024, 768], P('dp', 'seq'), may hold values from -6 to 6
- query_weight: bfloat16 [768, 384], replicated, may hold values from -0.3125 to 0.3125
- key_weight: bfloat16 [768, 384], replicated, may hold values from -0.21875 to 0.21875
- value_weight: bfloat16 [768, 384], replicated, may hold values from -0.21875 to 0.21875
- depth_weight: bfloat16 [9, 768], replicated, may hold values from -2 to 2
- point_weight: bfloat16 [768, 384], replicated, may hold values from -0.21875 to 0.21875
- kernel_weight: bfloat16 [384, 54], replicated, may hold values from -0.3125 to 0.3125
- convval_weight: bfloat16 [768, 384], replicated, may hold values from -0.21875 to 0.21875
- output_weight: bfloat16 [768, 768], replicated, may hold values from -0.875 to 0.875
- norm_gain: float32 [768], replicated, may hold values from 0.25 to 1.75
- norm_bias: float32 [768], replicated, may hold values from -1.5 to 1.5
- inner_weight: bfloat16 [2, 384, 1536], replicated, may hold values from -0.3125 to 0.3125
- outer_weight: bfloat16 [2, 1536, 384], replicated, may hold values from -0.15625 to 0.15625
- final_gain: float32 [768], replicated, may hold values from 0.25 to 1.75
- final_bias: float32 [768], replicated, may hold values from -1.5 to 1.5
Outputs:
- output: bfloat16 [24, 1024, 768], P('dp', 'seq')
- grad_input: bfloat16 [24, 1024, 768], P('dp', 'seq')
- grad_query: float32 [768, 384], P('seq')
- grad_key: float32 [768, 384], P('seq')
- grad_value: float32 [768, 384], P('seq')
- grad_depth: float32 [9, 768], P(None, 'seq')
- grad_point: float32 [768, 384], P('seq')
- grad_kernel: float32 [384, 54], P('seq')
- grad_convval: float32 [768, 384], P('seq')
- grad_output: float32 [768, 768], P('seq')
- grad_ngain: float32 [768], P('seq')
- grad_nbias: float32 [768], P('seq')
- grad_inner: float32 [2, 384, 1536], P(None, 'seq')
- grad_outer: float32 [2, 1536, 384], P(None, 'seq')
- grad_fgain: float32 [768], P('seq')
- grad_fbias: float32 [768], P('seq')
The draws below stay inside these ranges and needn't reach their ends.
Inputs may be any that keep to these rules, and one draw needn't show every extreme that they name: `lengths`: some sequence has all 1024 tokens valid.
All inputs are finite; a program needn't handle non-finite values.
Results may differ from the reference program's by a relative error of at most 0.015.
Values may be sent and summed in bfloat16 or wider, within the bound.
No kernel may reach another device: no remote copies, remote signals or barrier semaphores. Data moves between devices by JAX's collectives and lax.ppermute only.
A program may use at most 256 MiB of HBM per device.

```python
import jax
import jax.numpy as jnp
from jax import lax

D = 768
FF = 3072
HEADS = 6
HEAD_SIZE = 64
KERNEL = 9
GROUPS = 2
LENGTH = 1024
BATCH = 24
HALF = 384


def draw_lengths(key, part):
    first_key = jax.random.fold_in(key, 11)
    second_key = jax.random.fold_in(key, 23)
    lowest = min(40, LENGTH // 2)
    drawn = jax.random.randint(first_key, (BATCH,), lowest, LENGTH + 1, dtype=jnp.int32)
    chosen = jax.random.randint(second_key, (), 0, BATCH, dtype=jnp.int32)
    return drawn.at[chosen].set(LENGTH)


def levels(stream_key, extent, split, low, high):
    def one(axis_at, parts):
        steps = jax.random.uniform(jax.random.fold_in(jax.random.fold_in(stream_key, 6), axis_at), (parts,), jnp.float32, low / len(split), high / len(split))
        return jnp.repeat(jnp.exp(steps), extent[axis_at] // parts).reshape((-1,) + (1,) * (len(extent) - axis_at - 1))

    loudness = one(*split[0])
    for cut in split[1:]:
        loudness = loudness * one(*cut)
    return loudness


def normal_values(stream_key, shape, spread, limit, cuts=(), held_as=jnp.bfloat16):
    values = jax.random.normal(stream_key, shape, jnp.float32) * spread
    if len(cuts) > 0:
        values = levels(stream_key, shape, cuts, -0.22, 0.18) * values
    return jnp.clip(values, min=-limit, max=limit).astype(held_as)


def setup_inputs(seed: int = 0) -> dict:
    splits = jax.random.split(jax.random.key(seed), 18)
    hidden = normal_values(splits[0], (BATCH, LENGTH, D), 1.0, 6.0, ((0, 4), (1, 8)))
    lengths = draw_lengths(jax.random.fold_in(splits[17], 71), 0)
    cotangent = normal_values(splits[2], (BATCH, LENGTH, D), 1.0, 6.0, ((0, 4), (1, 8)))
    query_weight = normal_values(splits[3], (D, HALF), (D // 2) ** -0.5, 0.3125)
    key_weight = normal_values(splits[4], (D, HALF), D ** -0.5, 0.21875)
    value_weight = normal_values(splits[5], (D, HALF), D ** -0.5, 0.21875)
    depth_weight = normal_values(splits[6], (KERNEL, D), KERNEL ** -0.5, 2.0)
    point_weight = normal_values(splits[7], (D, HALF), D ** -0.5, 0.21875)
    kernel_weight = normal_values(splits[8], (HALF, HEADS * KERNEL), HALF ** -0.5, 0.3125)
    convval_weight = normal_values(splits[9], (D, HALF), D ** -0.5, 0.21875)
    output_weight = normal_values(splits[10], (2 * HALF, D), (D // 16) ** -0.5, 0.875)
    norm_gain = jnp.clip(1.0 + 0.15 * jax.random.normal(splits[11], (D,), jnp.float32), 0.25, 1.75)
    norm_bias = normal_values(splits[12], (D,), 0.3, 1.5, (), jnp.float32)
    inner_weight = normal_values(splits[13], (GROUPS, D // GROUPS, FF // GROUPS), (D // GROUPS) ** -0.5, 0.3125)
    outer_weight = normal_values(splits[14], (GROUPS, FF // GROUPS, D // GROUPS), (FF // GROUPS) ** -0.5, 0.15625)
    final_gain = jnp.clip(1.0 + 0.15 * jax.random.normal(splits[15], (D,), jnp.float32), 0.25, 1.75)
    final_bias = normal_values(splits[16], (D,), 0.3, 1.5, (), jnp.float32)
    return {"hidden": hidden, "lengths": lengths, "cotangent": cotangent, "query_weight": query_weight, "key_weight": key_weight, "value_weight": value_weight, "depth_weight": depth_weight, "point_weight": point_weight, "kernel_weight": kernel_weight, "convval_weight": convval_weight, "output_weight": output_weight, "norm_gain": norm_gain, "norm_bias": norm_bias, "inner_weight": inner_weight, "outer_weight": outer_weight, "final_gain": final_gain, "final_bias": final_bias}


@jax.custom_vjp
def low(v):
    return lax.optimization_barrier(v.astype(jnp.bfloat16)).astype(jnp.float32)

@jax.custom_vjp
def low_back(v):
    return v

def low_keep(v):
    return (low(v), None)

def low_pass(kept, grad):
    return (grad,)

def back_keep(v):
    return (v, None)

def back_low(kept, grad):
    return (low(grad),)
low.defvjp(low_keep, low_pass)
low_back.defvjp(back_keep, back_low)
HIGHEST = lax.Precision.HIGHEST
NEGATIVE = -1e+30

def rounded_both(values):
    return low_back(low(values))

def matmul(left_side, right_side):
    return jnp.dot(left_side, right_side, precision=HIGHEST)

def layer_norm(values, gain, shift):
    average = lax.optimization_barrier(jnp.mean(values, axis=-1, keepdims=True))
    centered = values - average
    variance = lax.optimization_barrier(jnp.mean(centered * centered, axis=-1, keepdims=True))
    return centered * lax.rsqrt(variance + 1e-12) * gain + shift

def grouped(values, weight):
    count = values.shape[0]
    pieces = values.reshape(count, weight.shape[0], weight.shape[1])
    return jnp.einsum('rgi,gio->rgo', pieces, weight, precision=HIGHEST).reshape(count, -1)

def forward(hidden, query_weight, key_weight, value_weight, depth_weight, point_weight, kernel_weight, convval_weight, output_weight, norm_gain, norm_bias, inner_weight, outer_weight, final_gain, final_bias, length):
    count = hidden.shape[0]
    reach = KERNEL // 2
    queries = rounded_both(matmul(hidden, query_weight))
    keys = rounded_both(matmul(hidden, key_weight))
    values = rounded_both(matmul(hidden, value_weight))
    convval = rounded_both(matmul(hidden, convval_weight))
    padded = jnp.pad(hidden, ((reach, reach), (0, 0)))
    depthwise = jnp.zeros_like(hidden)
    for offset in range(KERNEL):
        depthwise = depthwise + padded[offset:offset + count] * depth_weight[offset]
    depthwise = low(depthwise)
    key_conv = low_back(matmul(depthwise, point_weight))
    conv_query = low(key_conv * queries)
    logits = low_back(matmul(conv_query, kernel_weight)).reshape(count, HEADS, KERNEL)
    kernels = jax.nn.softmax(logits, axis=-1)
    conv_pad = jnp.pad(convval, ((reach, reach), (0, 0)))
    conv_out = jnp.zeros((count, HEADS, HEAD_SIZE), jnp.float32)
    for offset in range(KERNEL):
        window = conv_pad[offset:offset + count].reshape(count, HEADS, HEAD_SIZE)
        conv_out = conv_out + kernels[:, :, offset:offset + 1] * window
    conv_out = low(conv_out.reshape(count, HALF))
    query_heads = queries.reshape(count, HEADS, HEAD_SIZE)
    key_heads = keys.reshape(count, HEADS, HEAD_SIZE)
    value_heads = values.reshape(count, HEADS, HEAD_SIZE)
    scores = jnp.einsum('qhd,khd->hqk', query_heads, key_heads, precision=HIGHEST) * HEAD_SIZE ** (-0.5)
    valid = jnp.arange(count) < length
    scores = low_back(jnp.where(valid[None, None, :], scores, NEGATIVE))
    probs = rounded_both(jax.nn.softmax(scores, axis=-1))
    context = jnp.einsum('hqk,khd->qhd', probs, value_heads, precision=HIGHEST).reshape(count, HALF)
    context = rounded_both(context)
    joined = jnp.concatenate([context, conv_out], axis=1)
    summed = hidden + low_back(matmul(joined, output_weight))
    first = layer_norm(summed, norm_gain, norm_bias)
    inner = low_back(grouped(low(first), inner_weight))
    active = low(jax.nn.gelu(inner, approximate=False))
    total = first + low_back(grouped(active, outer_weight))
    return layer_norm(total, final_gain, final_bias)

def reference(hidden, lengths, cotangent, query_weight, key_weight, value_weight, depth_weight, point_weight, kernel_weight, convval_weight, output_weight, norm_gain, norm_bias, inner_weight, outer_weight, final_gain, final_bias):
    params = tuple((matrix.astype(jnp.float32) for matrix in (query_weight, key_weight, value_weight, depth_weight, point_weight, kernel_weight, convval_weight, output_weight, norm_gain, norm_bias, inner_weight, outer_weight, final_gain, final_bias)))

    def one_sequence(running, inputs):
        rows_in, length, cot_rows = inputs

        def apply(source, *weights):
            return forward(source, *weights, length)
        result, pullback = jax.vjp(apply, rows_in.astype(jnp.float32), *params)
        gradients = pullback(cot_rows.astype(jnp.float32))
        updated = tuple((before + addition for before, addition in zip(running, gradients[1:])))
        return (updated, (result.astype(jnp.bfloat16), gradients[0].astype(jnp.bfloat16)))
    zeros = tuple((jnp.zeros_like(matrix) for matrix in params))
    totals, outputs = lax.scan(one_sequence, zeros, (hidden, lengths, cotangent))
    return (outputs[0], outputs[1], totals[0], totals[1], totals[2], totals[3], totals[4], totals[5], totals[6], totals[7], totals[8], totals[9], totals[10], totals[11], totals[12], totals[13])
```

```python
import functools

import jax
import jax.numpy as jnp
from jax import lax
from jax.experimental import pallas as pl
from jax.experimental.pallas import tpu as pltpu
from jax.sharding import PartitionSpec as P

HEADS = 6
HEAD_SIZE = 64
KERNEL = 9
REACH = KERNEL // 2
PAD = 8
NEGATIVE = -1e30
GROUP = 2
SCALE = HEAD_SIZE ** (-0.5)
BF = jnp.bfloat16
F32 = jnp.float32


def dot(left, right):
    return jnp.dot(left, right, preferred_element_type=F32)


def dot_nt(left, right):
    return lax.dot_general(left, right, (((1,), (1,)), ((), ())), preferred_element_type=F32)


def dot_tn(left, right):
    return lax.dot_general(left, right, (((0,), (0,)), ((), ())), preferred_element_type=F32)


def stacked(pair):
    low_half = lax.broadcasted_iota(jnp.int32, pair.shape, 1) < HEAD_SIZE
    zero = jnp.zeros_like(pair)
    return jnp.concatenate([jnp.where(low_half, pair, zero), jnp.where(low_half, zero, pair)], axis=0)


def unstacked(trans):
    rows = trans.shape[1] // 2
    both = jnp.concatenate([trans[:HEAD_SIZE, :rows], trans[HEAD_SIZE:, rows:]], axis=0)
    return both.T


def fill_extended(x_ref, my, ext_ref):
    blocks, _, local, _ = x_ref.shape
    before = x_ref[jnp.maximum(my - 1, 0), 0, local - 16 : local, :].astype(F32)[16 - PAD :]
    after = x_ref[jnp.minimum(my + 1, blocks - 1), 0, 0:16, :].astype(F32)[:PAD]
    ext_ref[0:PAD, :] = jnp.where(my > 0, before, 0.0)
    ext_ref[PAD : PAD + local, :] = x_ref[my, 0].astype(F32)
    ext_ref[PAD + local : 2 * PAD + local, :] = jnp.where(my < blocks - 1, after, 0.0)


def forward_kernel(
    my_ref, len_ref, x_ref, wkv_ref, wqc_ref, dep_ref, wp_ref, wke_ref,
    kv_ref, q_ref, lse_ref, ka_ref, ca_ref, dw_ref, kern_ref, join_ref, cve_ref, xe_ref,
):
    blocks, _, local, width = x_ref.shape
    half = width // 2
    total = blocks * local
    my = my_ref[0]
    length = len_ref[pl.program_id(0)]
    kv_ref[0] = dot(x_ref[:, 0].reshape(total, width), wkv_ref[...]).astype(BF)
    fill_extended(x_ref, my, xe_ref)
    qc = dot(xe_ref[...].astype(BF), wqc_ref[...])
    queries = qc[PAD : PAD + local, :half].astype(BF)
    q_ref[0] = queries
    cve_ref[0] = qc[:, half:].astype(BF).astype(F32)
    depthwise = jnp.zeros((local, width), F32)
    for j in range(KERNEL):
        depthwise += xe_ref[PAD - REACH + j : PAD - REACH + j + local, :] * dep_ref[j : j + 1, :]
    dw = depthwise.astype(BF)
    dw_ref[0] = dw
    ka = dot(dw, wp_ref[...])
    ka_ref[0] = ka
    ca = (ka * queries.astype(F32)).astype(BF)
    ca_ref[0] = ca
    logits = dot(ca, wke_ref[...])
    parts = [logits[:, j * half : (j + 1) * half] for j in range(KERNEL)]
    top = functools.reduce(jnp.maximum, parts)
    parts = [jnp.exp(part - top) for part in parts]
    inverse = 1.0 / functools.reduce(jnp.add, parts)
    conv = jnp.zeros((local, half), F32)
    for j in range(KERNEL):
        kern = parts[j] * inverse
        kern_ref[0, :, j * half : (j + 1) * half] = kern
        conv += kern * cve_ref[0, PAD - REACH + j : PAD - REACH + j + local, :]
    join_ref[0, :, half:] = conv.astype(BF)
    valid = lax.broadcasted_iota(jnp.int32, (total, 1), 0) < length
    for pair in range(half // 128):
        lanes = slice(pair * 128, (pair + 1) * 128)
        vlanes = slice(half + pair * 128, half + (pair + 1) * 128)
        rows_q = stacked(queries[:, lanes]) * BF(SCALE)
        scores = jnp.where(valid, dot_nt(kv_ref[0, :, lanes], rows_q), NEGATIVE)
        highest = jnp.max(scores, axis=0, keepdims=True)
        expos = jnp.exp(scores - highest)
        totals = jnp.sum(expos, axis=0, keepdims=True)
        probs = (expos * (1.0 / totals)).astype(BF)
        lse_ref[0, pair : pair + 1, :] = highest + jnp.log(totals)
        context = unstacked(dot_tn(kv_ref[0, :, vlanes], probs))
        join_ref[0, :, lanes] = context.astype(BF)


def whole(shape):
    return pl.BlockSpec(shape, lambda *_: (0,) * len(shape), pipeline_mode=pl.Buffered(1))


def per_seq(*shape):
    return pl.BlockSpec((1,) + shape, lambda s, *_: (s,) + (0,) * len(shape))


def cost(flops, moved):
    return pl.CostEstimate(flops=int(flops), bytes_accessed=int(moved), transcendentals=0)


def run_forward(my, lengths, x_full, wkv, wqc, dep, wp, wke):
    blocks, seqs, local, width = x_full.shape
    half, total, ext = width // 2, blocks * local, local + 2 * PAD
    pairs = half // 128
    outs = [
        ((total, width), BF), ((local, half), BF), ((8, 2 * local), F32), ((local, half), F32), ((local, half), BF),
        ((local, width), BF), ((local, KERNEL * half), F32), ((local, width), BF), ((ext, half), F32),
    ]
    return pl.pallas_call(
        forward_kernel,
        out_shape=[jax.ShapeDtypeStruct((seqs,) + s, d) for s, d in outs],
        grid_spec=pltpu.PrefetchScalarGridSpec(
            num_scalar_prefetch=2,
            grid=(seqs,),
            in_specs=[pl.BlockSpec((blocks, 1, local, width), lambda s, *_: (0, s, 0, 0))]
            + [whole(w.shape) for w in (wkv, wqc, dep, wp, wke)],
            out_specs=[per_seq(*s) for s, _ in outs],
            scratch_shapes=[pltpu.VMEM((ext, width), F32)],
        ),
        compiler_params=pltpu.CompilerParams(vmem_limit_bytes=56 << 20),
        cost_estimate=cost(seqs * 6e9, seqs * 8e6),
        name="fwd_mix",
    )(my, lengths, x_full, wkv, wqc, dep, wp, wke)


def norm_parts(values):
    mean = jnp.mean(values, axis=-1, keepdims=True)
    centered = values - mean
    inv = lax.rsqrt(jnp.mean(centered * centered, axis=-1, keepdims=True) + 1e-12)
    return centered * inv, inv


def norm_back(grad, normed, inv, gain):
    e = grad * gain
    return inv * (
        e - jnp.mean(e, axis=-1, keepdims=True) - normed * jnp.mean(e * normed, axis=-1, keepdims=True)
    )


def mlp_kernel(
    x_ref, join_ref, cot_ref, wo_ref, inner_ref, outer_ref, vec_ref,
    out_ref, dhs_ref, dctx_ref, dco_ref, act_ref, dpre_ref, h1b_ref, dout_ref, dproj_ref, sums_ref, slope_ref,
):
    groups, gin, gff = inner_ref.shape
    half = dctx_ref.shape[1]
    ngain, nbias = vec_ref[0:1, :], vec_ref[1:2, :]
    fgain, fbias = vec_ref[2:3, :], vec_ref[3:4, :]
    hsum = x_ref[...].astype(F32) + dot(join_ref[...], wo_ref[...])
    n1, r1 = norm_parts(hsum)
    h1 = n1 * ngain + nbias
    h1b = h1.astype(BF)
    h1b_ref[...] = h1b
    ffn = []
    for g in range(groups):
        pre = dot(h1b[:, g * gin : (g + 1) * gin], inner_ref[g])
        cdf = 0.5 + 0.5 * lax.erf(pre * (2.0**-0.5))
        slope_ref[g] = cdf + pre * (jnp.exp(-0.5 * pre * pre) * 0.3989422804014327)
        act = (pre * cdf).astype(BF)
        act_ref[:, g * gff : (g + 1) * gff] = act
        ffn.append(dot(act, outer_ref[g]))
    n2, r2 = norm_parts(h1 + jnp.concatenate(ffn, axis=1))
    out_ref[...] = (n2 * fgain + fbias).astype(BF)
    cot = cot_ref[...].astype(F32)
    dz = norm_back(cot, n2, r2, fgain)
    dout = dz.astype(BF)
    dout_ref[...] = dout
    back = []
    for g in range(groups):
        dact = dot_nt(dout[:, g * gin : (g + 1) * gin], outer_ref[g])
        dpre = (dact * slope_ref[g]).astype(BF)
        dpre_ref[:, g * gff : (g + 1) * gff] = dpre
        back.append(dot_nt(dpre, inner_ref[g]))
    dh1 = dz + jnp.concatenate(back, axis=1)
    dhs = norm_back(dh1, n1, r1, ngain)
    dhs_ref[...] = dhs
    dproj = dhs.astype(BF)
    dproj_ref[...] = dproj
    dcat = dot_nt(dproj, wo_ref[...])
    dctx_ref[...] = dcat[:, :half].astype(BF)
    dco_ref[...] = dcat[:, half:]
    sums = [
        jnp.sum(v, axis=0, keepdims=True) for v in (dh1 * n1, dh1, cot * n2, cot)
    ]
    sums_ref[...] = jnp.concatenate(sums + [jnp.zeros((4, hsum.shape[1]), F32)], axis=0)


def run_mlp(x, joined, cot, wo, inner, outer, vecs):
    rows, width = x.shape
    ff = inner.shape[0] * inner.shape[2]
    half = width // 2
    outs = [
        ((rows, width), BF), ((rows, width), F32), ((rows, half), BF), ((rows, half), F32), ((rows, ff), BF),
        ((rows, ff), BF), ((rows, width), BF), ((rows, width), BF), ((rows, width), BF), ((8, width), F32),
    ]
    ins = (x, joined, cot, wo, inner, outer, vecs)
    return pl.pallas_call(
        mlp_kernel,
        out_shape=[jax.ShapeDtypeStruct(s, d) for s, d in outs],
        grid=(1,),
        in_specs=[whole(a.shape) for a in ins],
        out_specs=[whole(s) for s, _ in outs],
        scratch_shapes=[pltpu.VMEM((inner.shape[0], rows, inner.shape[2]), F32)],
        compiler_params=pltpu.CompilerParams(vmem_limit_bytes=56 << 20),
        cost_estimate=cost(6e9, 20e6),
        name="mlp_both",
    )(*ins)


def backward_kernel(
    my_ref, len_ref, x_ref, kv_ref, q_ref, lse_ref, ka_ref, kern_ref, cve_ref, dctx_ref, dco_ref, dhs_ref,
    wkv_ref, wqc_ref, dep_ref, wp_ref, kw_ref, ones_ref, sel_ref,
    part_ref, own_ref, dkv_ref, dq_ref, dcve_ref, xe_ref, dka_ref, dlog_ref, gdep_ref,
    xes_ref, dxe_ref, dce_ref, full_ref,
):
    blocks, _, local, width = x_ref.shape
    half = width // 2
    total = blocks * local
    my = my_ref[0]
    length = len_ref[pl.program_id(0)]
    queries = q_ref[0]
    valid = lax.broadcasted_iota(jnp.int32, (total, 1), 0) < length
    dq_parts = []
    for pair in range(half // 128):
        lanes = slice(pair * 128, (pair + 1) * 128)
        vlanes = slice(half + pair * 128, half + (pair + 1) * 128)
        rows_q = stacked(queries[:, lanes]) * BF(SCALE)
        rows_d = stacked(dctx_ref[0, :, lanes])
        scores = jnp.where(valid, dot_nt(kv_ref[0, :, lanes], rows_q), NEGATIVE)
        probs = jnp.exp(scores - lse_ref[0, pair : pair + 1, :])
        dprobs = dot_nt(kv_ref[0, :, vlanes], rows_d).astype(BF).astype(F32)
        weighted = jnp.sum(probs * dprobs, axis=0, keepdims=True)
        dscores = (probs * (dprobs - weighted)).astype(BF)
        dkv_ref[0, :, lanes] = dot(dscores, rows_q).astype(BF)
        dkv_ref[0, :, vlanes] = dot(probs.astype(BF), rows_d).astype(BF)
        dq_parts.append(unstacked(dot_tn(kv_ref[0, :, lanes], dscores)))
    dq_att = jnp.concatenate(dq_parts, axis=1) * SCALE
    dco = dco_ref[0]
    dce_ref[...] = jnp.zeros_like(dce_ref)
    dkerns = []
    shared = jnp.zeros((local, half), F32)
    for j in range(KERNEL):
        rows = slice(PAD - REACH + j, PAD - REACH + j + local)
        kern = kern_ref[0, :, j * half : (j + 1) * half]
        dce_ref[rows, :] += kern * dco
        product = dco * cve_ref[0, rows, :]
        high = product.astype(BF)
        rest = (product - high.astype(F32)).astype(BF)
        dkern = dot(high, ones_ref[...]) + dot(rest, ones_ref[...])
        shared += kern * dkern
        dkerns.append(dkern)
    compact = jnp.zeros((local, 128), F32)
    for j in range(KERNEL):
        kern = kern_ref[0, :, j * half : (j + 1) * half]
        dlog = (kern * (dkerns[j] - shared)).astype(BF)
        compact += dot(dlog, sel_ref[j])
    dlog_low = compact.astype(BF)
    dlog_ref[0] = dlog_low
    dca = dot_nt(dlog_low, kw_ref[...])
    dka = (dca * queries.astype(F32)).astype(BF)
    dka_ref[0] = dka
    dq = (dq_att + dca * ka_ref[0]).astype(BF)
    dq_ref[0] = dq
    fill_extended(x_ref, my, xes_ref)
    xe_ref[0] = xes_ref[...].astype(BF)
    ddw = dot_nt(dka, wp_ref[...])
    dxe_ref[...] = jnp.zeros_like(dxe_ref)
    taps = []
    for j in range(KERNEL):
        rows = slice(PAD - REACH + j, PAD - REACH + j + local)
        taps.append(jnp.sum(ddw * xes_ref[rows, :], axis=0, keepdims=True))
        dxe_ref[rows, :] += ddw * dep_ref[j : j + 1, :]
    taps.append(jnp.zeros((16 - KERNEL, width), F32))
    gdep_ref[0] = jnp.concatenate(taps, axis=0)
    at = lax.broadcasted_iota(jnp.int32, (local + 2 * PAD, 1), 0) + my * local - PAD
    inside = (at >= 0) & (at < total)
    dcve = jnp.where(inside, dce_ref[...], 0.0).astype(BF)
    dcve_ref[0] = dcve
    dxe_ref[...] += dot_nt(dcve, wqc_ref[:, half:])
    own_ref[0] = dhs_ref[0] + dxe_ref[PAD : PAD + local, :] + dot_nt(dq, wqc_ref[:, :half])
    for b in range(blocks):
        full_ref[b] = dot_nt(dkv_ref[0, b * local : (b + 1) * local, :], wkv_ref[...])

    @pl.when(my > 0)
    def _():
        full_ref[my - 1, local - PAD : local, :] += dxe_ref[0:PAD, :]

    @pl.when(my < blocks - 1)
    def _():
        full_ref[my + 1, 0:PAD, :] += dxe_ref[PAD + local :, :]

    part_ref[:, 0] = full_ref[...].astype(BF)


def run_backward(my, lengths, x_full, saved, grads, weights):
    blocks, seqs, local, width = x_full.shape
    half, total, ext = width // 2, blocks * local, local + 2 * PAD
    outs = [
        ((local, width), F32), ((total, width), BF), ((local, half), BF), ((ext, half), BF), ((ext, width), BF),
        ((local, half), BF), ((local, 128), BF), ((16, width), F32),
    ]
    block = pl.BlockSpec((blocks, 1, local, width), lambda s, *_: (0, s, 0, 0))
    return pl.pallas_call(
        backward_kernel,
        out_shape=[jax.ShapeDtypeStruct((blocks, seqs, local, width), BF)]
        + [jax.ShapeDtypeStruct((seqs,) + s, d) for s, d in outs],
        grid_spec=pltpu.PrefetchScalarGridSpec(
            num_scalar_prefetch=2,
            grid=(seqs,),
            in_specs=[block] + [per_seq(*a.shape[1:]) for a in (*saved, *grads)] + [whole(w.shape) for w in weights],
            out_specs=[block] + [per_seq(*s) for s, _ in outs],
            scratch_shapes=[
                pltpu.VMEM((ext, width), F32),
                pltpu.VMEM((ext, width), F32),
                pltpu.VMEM((ext, half), F32),
                pltpu.VMEM((blocks, local, width), F32),
            ],
        ),
        compiler_params=pltpu.CompilerParams(vmem_limit_bytes=60 << 20),
        cost_estimate=cost(seqs * 8e9, seqs * 10e6),
        name="bwd_mix",
    )(my, lengths, x_full, *saved, *grads, *weights)


def peers(value, axis, step):
    count = lax.axis_size(axis)
    return lax.ppermute(value, axis, [(i, i ^ step) for i in range(count)])


def scatter_direct(value, axis, steps, index):
    total = lax.dynamic_index_in_dim(value, index, 0, keepdims=False).astype(F32)
    for step, unit in steps:
        piece = lax.dynamic_index_in_dim(value, index ^ step, 0, keepdims=False)
        total = total + peers(piece, axis, step * unit).astype(F32)
    return total


def reduce_shares(packed):
    n_seq, n_dp = lax.axis_size("seq"), lax.axis_size("dp")
    rows, lanes = packed.shape[1:]
    seq, dp = lax.axis_index("seq"), lax.axis_index("dp")
    core, far = seq % 2, seq // 2
    split = packed.reshape(n_seq // 2, 2, rows, lanes).swapaxes(0, 1)
    near = scatter_direct(split, "seq", [(1, 1)], core).astype(BF)
    near = near.reshape(n_seq // 2, n_dp, rows // n_dp, lanes).swapaxes(0, 1)
    mid = scatter_direct(near, "dp", [(k, 1) for k in range(1, n_dp)], dp).astype(BF)
    mine = scatter_direct(mid, "seq", [(k, 2) for k in range(1, n_seq // 2)], far).astype(BF)
    return lax.all_gather(mine, "dp", axis=0, tiled=True).astype(F32)


def body(
    hidden, lengths, cotangent, query_weight, key_weight, value_weight, depth_weight, point_weight, kernel_weight,
    convval_weight, output_weight, norm_gain, norm_bias, inner_weight, outer_weight, final_gain, final_bias,
):
    seqs, local, width = hidden.shape
    half = width // 2
    n_seq, n_dp = lax.axis_size("seq"), lax.axis_size("dp")
    my = lax.axis_index("seq").reshape(1).astype(jnp.int32)
    groups = seqs // GROUP
    cut = lambda a, g: a[g * GROUP : (g + 1) * GROUP]
    x_full = [lax.all_gather(cut(hidden, g), "seq") for g in range(groups)]

    wkv = jnp.concatenate([key_weight, value_weight], axis=1)
    wqc = jnp.concatenate([query_weight, convval_weight], axis=1)
    dep = jnp.pad(depth_weight.astype(F32), ((0, 16 - KERNEL), (0, 0)))
    by_tap = kernel_weight.reshape(half, HEADS, KERNEL).swapaxes(1, 2)
    wke = jnp.repeat(by_tap, HEAD_SIZE, axis=2).reshape(half, KERNEL * half)
    kw = jnp.pad(kernel_weight, ((0, 0), (0, 128 - HEADS * KERNEL)))
    lane = jnp.arange(half)
    ones = (lane[:, None] // HEAD_SIZE == lane[None, :] // HEAD_SIZE).astype(BF)
    column = jnp.where(lane % HEAD_SIZE == 0, lane // HEAD_SIZE * KERNEL, -128)
    sel = (column[None, :, None] + jnp.arange(KERNEL)[:, None, None] == jnp.arange(128)[None, None, :]).astype(BF)
    vecs = jnp.stack([norm_gain, norm_bias, final_gain, final_bias] * 2)

    kept, mlps, backs, shares = [], [], [], []
    for g in range(groups):
        lens = cut(lengths, g)
        kv, q, lse, ka, ca, dw, kern, joined, cve = run_forward(my, lens, x_full[g], wkv, wqc, dep, point_weight, wke)
        flat = lambda a: a.reshape(GROUP * local, -1)
        mlp = run_mlp(
            flat(cut(hidden, g)), flat(joined), flat(cut(cotangent, g)), output_weight, inner_weight, outer_weight, vecs
        )
        out, dhs, dctx, dco = (a.reshape(GROUP, local, -1) for a in mlp[:4])
        back = run_backward(
            my, lens, x_full[g], (kv, q, lse, ka, kern, cve), (dctx, dco, dhs),
            (wkv, wqc, dep, point_weight, kw, ones, sel),
        )
        shares.append(lax.psum_scatter(back[0], "seq", scatter_dimension=0))
        kept.append((ca, dw, joined))
        mlps.append((out, *mlp[4:]))
        backs.append(back[1:])

    join = lambda parts: jnp.concatenate([p.reshape(-1, p.shape[-1]) for p in parts], axis=0)
    output = jnp.concatenate([m[0] for m in mlps], axis=0)
    grad_input = jnp.concatenate(
        [(b[0] + s.astype(F32)).astype(BF) for b, s in zip(backs, shares)], axis=0
    )
    ca, dw, joined = (join([k[i] for k in kept]) for i in range(3))
    act, dpre, h1b, dout, dproj = (join([m[i] for m in mlps]) for i in range(1, 6))
    sums = functools.reduce(jnp.add, [m[6] for m in mlps])[:4]
    dkv, dq, dcve, xe, dka, dlog = (join([b[i] for b in backs]) for i in range(1, 7))
    gdep = functools.reduce(jnp.add, [b[7][s] for b in backs for s in range(GROUP)])[:KERNEL]
    everything = jnp.concatenate([x.swapaxes(0, 1).reshape(-1, width) for x in x_full], axis=0)
    flat_x = hidden.reshape(seqs * local, width)
    grad_kv = dot_tn(everything, dkv)
    grad_query = dot_tn(flat_x, dq)
    grad_convval = dot_tn(xe, dcve)
    grad_point = dot_tn(dw, dka)
    grad_kernel = dot_tn(ca, dlog)
    grad_output = dot_tn(joined, dproj)
    n_groups, gin, gff = inner_weight.shape
    grad_inner = jnp.stack(
        [dot_tn(h1b[:, i * gin : (i + 1) * gin], dpre[:, i * gff : (i + 1) * gff]) for i in range(n_groups)]
    )
    grad_outer = jnp.stack(
        [dot_tn(act[:, i * gff : (i + 1) * gff], dout[:, i * gin : (i + 1) * gin]) for i in range(n_groups)]
    )

    def piece(a, lanes):
        a = a.reshape(n_seq, a.shape[0] // n_seq, a.shape[1])
        return [a[:, :, i : i + lanes] for i in range(0, a.shape[2], lanes)]

    small = jnp.concatenate([gdep, sums], axis=0)
    small = small.reshape(small.shape[0], n_seq, width // n_seq).swapaxes(0, 1)
    small_rows = 16
    small = jnp.pad(small, ((0, 0), (0, small_rows - small.shape[1]), (0, half - small.shape[2])))
    kernel_pad = jnp.pad(grad_kernel, ((0, 0), (0, half - grad_kernel.shape[1]))).reshape(n_seq, -1, half)
    pieces = (
        piece(grad_query, half) + piece(grad_kv, half) + piece(grad_convval, half) + piece(grad_point, half)
        + piece(grad_output, half)
        + [p for i in range(n_groups) for p in piece(grad_inner[i], half)]
        + [p for i in range(n_groups) for p in piece(grad_outer[i], half)]
        + [kernel_pad, small]
    )
    counts = [p.shape[1] for p in pieces]
    total_rows = sum(counts)
    padded = -(-total_rows // (16 * n_dp)) * 16 * n_dp
    packed = jnp.concatenate([p.astype(BF) for p in pieces], axis=1)
    packed = jnp.pad(packed, ((0, 0), (0, padded - total_rows), (0, 0)))
    reduced = reduce_shares(packed)
    got, at = [], 0
    for rows in counts:
        got.append(reduced[at : at + rows])
        at += rows
    take = iter(got)
    r_query, r_key, r_value, r_convval, r_point = (next(take) for _ in range(5))
    r_output = jnp.concatenate([next(take) for _ in range(2)], axis=1)
    per = gff // half
    r_inner = jnp.stack([jnp.concatenate([next(take) for _ in range(per)], axis=1) for _ in range(n_groups)])
    r_outer = jnp.stack([next(take) for _ in range(n_groups)])
    r_kernel = next(take)[:, : HEADS * KERNEL]
    r_small = next(take)[:, : width // n_seq]
    r_depth = r_small[:KERNEL]
    r_ngain, r_nbias, r_fgain, r_fbias = (r_small[KERNEL + i] for i in range(4))
    return (
        output, grad_input, r_query, r_key, r_value, r_depth, r_point, r_kernel, r_convval, r_output, r_ngain, r_nbias,
        r_inner, r_outer, r_fgain, r_fbias,
    )


def solution(mesh):
    rows = P("dp", "seq", None)
    return jax.shard_map(
        body,
        mesh=mesh,
        in_specs=(rows, P("dp"), rows) + (P(),) * 14,
        out_specs=(rows, rows)
        + (P("seq", None),) * 3
        + (P(None, "seq"),)
        + (P("seq", None),) * 4
        + (P("seq"),) * 2
        + (P(None, "seq", None),) * 2
        + (P("seq"),) * 2,
        check_vma=False,
    )
```

```python
import functools

import jax
import jax.numpy as jnp
from jax import lax
from jax.experimental import pallas as pl
from jax.experimental.pallas import tpu as pltpu
from jax.sharding import PartitionSpec as P

HEADS = 6
HEAD_SIZE = 64
KERNEL = 9
REACH = KERNEL // 2
PAD = 8
NEGATIVE = -1e30
GROUP = 2
SCALE = HEAD_SIZE ** (-0.5)
BF = jnp.bfloat16
F32 = jnp.float32
UNIT = 48
QUARTERS = 4
MIB = 1 << 20
VMEM = 36


def dot(left, right):
    return jnp.dot(left, right, preferred_element_type=F32)


def dot_nt(left, right):
    return lax.dot_general(left, right, (((1,), (1,)), ((), ())), preferred_element_type=F32)


def dot_tn(left, right):
    return lax.dot_general(left, right, (((0,), (0,)), ((), ())), preferred_element_type=F32)


def stacked(pair):
    low_half = lax.broadcasted_iota(jnp.int32, pair.shape, 1) < HEAD_SIZE
    zero = jnp.zeros_like(pair)
    return jnp.concatenate([jnp.where(low_half, pair, zero), jnp.where(low_half, zero, pair)], axis=0)


def unstacked(trans):
    rows = trans.shape[1] // 2
    both = jnp.concatenate([trans[:HEAD_SIZE, :rows], trans[HEAD_SIZE:, rows:]], axis=0)
    return both.T


def whole(shape):
    return pl.BlockSpec(shape, lambda *_: (0,) * len(shape), pipeline_mode=pl.Buffered(1))


def per_seq(*shape):
    return pl.BlockSpec((1,) + shape, lambda s, *_: (s,) + (0,) * len(shape))


def shaped(shape, dtype, big=False):
    return pltpu.HBM(shape, dtype) if big else jax.ShapeDtypeStruct(shape, dtype)


def in_hbm(value):
    return pltpu.with_memory_space_constraint(value, pltpu.HBM)


def cost(micros):
    return pl.CostEstimate(flops=int(micros * 1.1e9), bytes_accessed=int(micros * 1e6), transcendentals=0)


def params(mib):
    return pltpu.CompilerParams(vmem_limit_bytes=mib * MIB)


def fill_extended(before_ref, x_ref, after_ref, ext_ref):
    local = x_ref.shape[1]
    ext_ref[0:PAD, :] = before_ref[0].astype(F32)
    ext_ref[PAD : PAD + local, :] = x_ref[0].astype(F32)
    ext_ref[PAD + local :, :] = after_ref[0].astype(F32)


def conv_forward_kernel(
    before_ref, x_ref, after_ref, wq_ref, wc_ref, dep_ref, wp_ref, wke_ref,
    q_ref, ka_ref, ca_ref, dw_ref, kern_ref, co_ref, cve_ref, xe_ref,
):
    local, half = x_ref.shape[1], wq_ref.shape[1]
    fill_extended(before_ref, x_ref, after_ref, xe_ref)
    queries = dot(x_ref[0], wq_ref[...]).astype(BF)
    q_ref[0] = queries
    cve_ref[0] = dot(xe_ref[...].astype(BF), wc_ref[...]).astype(BF).astype(F32)
    depthwise = jnp.zeros((local, x_ref.shape[2]), F32)
    for j in range(KERNEL):
        depthwise += xe_ref[PAD - REACH + j : PAD - REACH + j + local, :] * dep_ref[j : j + 1, :]
    dw = depthwise.astype(BF)
    dw_ref[0] = dw
    ka = dot(dw, wp_ref[...])
    ka_ref[0] = ka
    ca = (ka * queries.astype(F32)).astype(BF)
    ca_ref[0] = ca
    logits = dot(ca, wke_ref[...])
    parts = [logits[:, j * half : (j + 1) * half] for j in range(KERNEL)]
    top = functools.reduce(jnp.maximum, parts)
    parts = [jnp.exp(part - top) for part in parts]
    inverse = 1.0 / functools.reduce(jnp.add, parts)
    conv = jnp.zeros((local, half), F32)
    for j in range(KERNEL):
        kern = parts[j] * inverse
        kern_ref[0, :, j * half : (j + 1) * half] = kern
        conv += kern * cve_ref[0, PAD - REACH + j : PAD - REACH + j + local, :]
    co_ref[0] = conv.astype(BF)


def run_conv_forward(before, x, after, wq, wc, dep, wp, wke):
    seqs, local, width = x.shape
    half, ext = width // 2, local + 2 * PAD
    outs = [
        ((local, half), BF), ((local, half), F32), ((local, half), BF), ((local, width), BF),
        ((local, KERNEL * half), F32), ((local, half), BF), ((ext, half), F32),
    ]
    return pl.pallas_call(
        conv_forward_kernel,
        out_shape=[shaped((seqs,) + s, d, s[-1] > width) for s, d in outs],
        grid=(seqs,),
        in_specs=[per_seq(PAD, width), per_seq(local, width), per_seq(PAD, width)]
        + [whole(w.shape) for w in (wq, wc, dep, wp, wke)],
        out_specs=[per_seq(*s) for s, _ in outs],
        scratch_shapes=[pltpu.VMEM((ext, width), F32)],
        compiler_params=params(VMEM),
        cost_estimate=cost(13),
        name="conv_fwd",
    )(before, x, after, wq, wc, dep, wp, wke)


def chunk_rows(place_ref, i, local):
    n = place_ref.shape[0]
    low, high = place_ref[i] * local, place_ref[n // 2 + i] * local
    return low, high, jnp.minimum(low, high)


def valid_rows(low, high, local, length):
    row = lax.broadcasted_iota(jnp.int32, (2 * local, 1), 0)
    return jnp.where(row < local, row + low, row + (high - local)) < length


def attend_kernel(
    first, place_ref, len_ref, near_ref, far_ref, q_ref, wk_ref, wv_ref,
    kv_ref, lse_ref, ctx_ref, low_ref, top_ref, sum_ref, acc_ref,
):
    chunks, _, local, width = near_ref.shape
    half = width // 2
    pairs = half // 128
    length = len_ref[first + pl.program_id(0)]
    top_ref[...] = jnp.full_like(top_ref, NEGATIVE)
    sum_ref[...] = jnp.zeros_like(sum_ref)
    acc_ref[...] = jnp.zeros_like(acc_ref)
    rows_q = [stacked(q_ref[0, :, p * 128 : (p + 1) * 128]) * BF(SCALE) for p in range(pairs)]

    @pl.loop(0, chunks)
    def _(i):
        low, high, start = chunk_rows(place_ref, i, local)

        @pl.when(start < length)
        def _():
            x = jnp.concatenate([near_ref[i, 0], far_ref[i, 0]], axis=0)
            kv_ref[0, i, :, :half] = dot(x, wk_ref[...]).astype(BF)
            kv_ref[0, i, :, half:] = dot(x, wv_ref[...]).astype(BF)
            valid = valid_rows(low, high, local, length)
            for p in range(pairs):
                lanes = slice(p * 128, (p + 1) * 128)
                vlanes = slice(half + p * 128, half + (p + 1) * 128)
                scores = jnp.where(valid, dot_nt(kv_ref[0, i, :, lanes], rows_q[p]), NEGATIVE)
                old = top_ref[p : p + 1, :]
                top = jnp.maximum(old, jnp.max(scores, axis=0, keepdims=True))
                expos = jnp.exp(scores - top)
                fade = jnp.exp(old - top)
                top_ref[p : p + 1, :] = top
                sum_ref[p : p + 1, :] = sum_ref[p : p + 1, :] * fade + jnp.sum(expos, axis=0, keepdims=True)
                acc_ref[p] = acc_ref[p] * fade + dot_tn(kv_ref[0, i, :, vlanes], expos.astype(BF))

    for p in range(pairs):
        totals = sum_ref[p : p + 1, :]
        lse_ref[0, p : p + 1, :] = top_ref[p : p + 1, :] + jnp.log(totals)
        context = unstacked(acc_ref[p] * (1.0 / totals))
        ctx_ref[0, :, p * 128 : (p + 1) * 128] = context
        low_ref[0, :, p * 128 : (p + 1) * 128] = context.astype(BF)


def run_attend(place, lengths, first, near, far, q, wk, wv):
    chunks, _, local, width = near.shape
    half, seqs = width // 2, GROUP
    pairs = half // 128
    outs = [((chunks, 2 * local, width), BF), ((8, 2 * local), F32), ((local, half), F32), ((local, half), BF)]
    block = pl.BlockSpec((chunks, 1, local, width), lambda s, *_: (0, s, 0, 0))
    return pl.pallas_call(
        functools.partial(attend_kernel, first),
        out_shape=[shaped((seqs,) + s, d, len(s) > 2) for s, d in outs],
        grid_spec=pltpu.PrefetchScalarGridSpec(
            num_scalar_prefetch=2,
            grid=(seqs,),
            in_specs=[block, block, pl.BlockSpec((1, local, half), lambda s, *_: (s + first, 0, 0))]
            + [whole(wk.shape), whole(wv.shape)],
            out_specs=[per_seq(*s) for s, _ in outs],
            scratch_shapes=[
                pltpu.VMEM((8, 2 * local), F32),
                pltpu.VMEM((8, 2 * local), F32),
                pltpu.VMEM((pairs, 128, 2 * local), F32),
            ],
        ),
        compiler_params=params(VMEM),
        cost_estimate=cost(12),
        name="attn_fwd",
    )(place, lengths, in_hbm(near), in_hbm(far), q, wk, wv)


def norm_parts(values):
    mean = jnp.mean(values, axis=-1, keepdims=True)
    centered = values - mean
    inv = lax.rsqrt(jnp.mean(centered * centered, axis=-1, keepdims=True) + 1e-12)
    return centered * inv, inv


def norm_back(grad, normed, inv, gain):
    e = grad * gain
    return inv * (
        e - jnp.mean(e, axis=-1, keepdims=True) - normed * jnp.mean(e * normed, axis=-1, keepdims=True)
    )


def normal_cdf(values):
    bell = jnp.exp(values * values * -0.5)
    t = 1.0 / (1.0 + jnp.abs(values) * (0.3275911 * 2.0**-0.5))
    poly = 0.5 * 1.061405429
    for coef in (-1.453152027, 1.421413741, -0.284496736, 0.254829592):
        poly = poly * t + 0.5 * coef
    tail = poly * t * bell
    return jnp.where(values < 0.0, tail, 1.0 - tail), bell


def mlp_kernel(
    x_ref, ctx_ref, co_ref, cot_ref, vec_ref, wo_hbm, inner_hbm, outer_hbm,
    out_ref, dhs_ref, dctx_ref, dco_ref, h1b_ref, dout_ref, dproj_ref, sums_ref, act_hbm, dpre_hbm,
    slope_ref, wo_ref, inner_ref, outer_ref, act_ref, dpre_ref, in_sem, out_sem,
):
    groups, gin, gff = inner_ref.shape
    half = dctx_ref.shape[1]
    loads = [pltpu.make_async_copy(wo_hbm, wo_ref, in_sem.at[0])]
    for g in range(groups):
        loads.append(pltpu.make_async_copy(inner_hbm.at[g], inner_ref.at[g], in_sem.at[1 + 2 * g]))
        loads.append(pltpu.make_async_copy(outer_hbm.at[g], outer_ref.at[g], in_sem.at[2 + 2 * g]))
    loads[0].start()
    stores = []
    for i, (source, target) in enumerate(((act_ref, act_hbm), (dpre_ref, dpre_hbm))):
        for g in range(groups):
            lanes = pl.ds(g * gff, gff)
            stores.append(
                pltpu.make_async_copy(source.at[:, lanes], target.at[:, lanes], out_sem.at[i * groups + g])
            )
    loads[0].wait()
    for load in loads[1:]:
        load.start()
    ngain, nbias = vec_ref[0:1, :], vec_ref[1:2, :]
    fgain, fbias = vec_ref[2:3, :], vec_ref[3:4, :]
    hsum = x_ref[...].astype(F32) + dot(ctx_ref[...], wo_ref[:half, :]) + dot(co_ref[...], wo_ref[half:, :])
    n1, r1 = norm_parts(hsum)
    h1 = n1 * ngain + nbias
    h1b = h1.astype(BF)
    h1b_ref[...] = h1b
    ffn = []
    for g in range(groups):
        loads[1 + 2 * g].wait()
        pre = dot(h1b[:, g * gin : (g + 1) * gin], inner_ref[g])
        cdf, bell = normal_cdf(pre)
        slope_ref[g] = cdf + pre * (bell * 0.3989422804014327)
        act = (pre * cdf).astype(BF)
        act_ref[:, g * gff : (g + 1) * gff] = act
        stores[g].start()
        loads[2 + 2 * g].wait()
        ffn.append(dot(act, outer_ref[g]))
    n2, r2 = norm_parts(h1 + jnp.concatenate(ffn, axis=1))
    out_ref[...] = (n2 * fgain + fbias).astype(BF)
    cot = cot_ref[...].astype(F32)
    dz = norm_back(cot, n2, r2, fgain)
    dout = dz.astype(BF)
    dout_ref[...] = dout
    back = []
    for g in range(groups):
        dact = dot_nt(dout[:, g * gin : (g + 1) * gin], outer_ref[g])
        dpre = (dact * slope_ref[g]).astype(BF)
        dpre_ref[:, g * gff : (g + 1) * gff] = dpre
        stores[groups + g].start()
        back.append(dot_nt(dpre, inner_ref[g]))
    dh1 = dz + jnp.concatenate(back, axis=1)
    dhs = norm_back(dh1, n1, r1, ngain)
    dhs_ref[...] = dhs
    dproj = dhs.astype(BF)
    dproj_ref[...] = dproj
    dctx_ref[...] = dot_nt(dproj, wo_ref[:half, :]).astype(BF)
    dco_ref[...] = dot_nt(dproj, wo_ref[half:, :])
    sums = [jnp.sum(v, axis=0, keepdims=True) for v in (dh1 * n1, dh1, cot * n2, cot)]
    sums_ref[...] = jnp.concatenate(sums + [jnp.zeros((4, hsum.shape[1]), F32)], axis=0)
    for store in stores:
        store.wait()


def run_mlp(g, x, ctx, co, cot, wo, inner, outer, vecs):
    rows, half = ctx.shape
    width = 2 * half
    ff = inner.shape[0] * inner.shape[2]
    outs = [
        ((rows, width), BF), ((rows, width), F32), ((rows, half), BF), ((rows, half), F32),
        ((rows, width), BF), ((rows, width), BF), ((rows, width), BF), ((8, width), F32),
    ]
    hbm = pl.BlockSpec(memory_space=pltpu.HBM)
    groups = inner.shape[0]
    part = lambda lanes: pl.BlockSpec((rows, lanes), lambda _: (g, 0), pipeline_mode=pl.Buffered(1))
    return pl.pallas_call(
        mlp_kernel,
        out_shape=[jax.ShapeDtypeStruct(s, d) for s, d in outs] + [jax.ShapeDtypeStruct((rows, ff), BF)] * 2,
        grid=(1,),
        in_specs=[part(width), whole(ctx.shape), part(half), part(width), whole(vecs.shape)] + [hbm] * 3,
        out_specs=[whole(s) for s, _ in outs] + [hbm] * 2,
        scratch_shapes=[
            pltpu.VMEM((groups, rows, inner.shape[2]), F32),
            *(pltpu.VMEM(w.shape, BF) for w in (wo, inner, outer)),
            pltpu.VMEM((rows, ff), BF),
            pltpu.VMEM((rows, ff), BF),
            pltpu.SemaphoreType.DMA((1 + 2 * groups,)),
            pltpu.SemaphoreType.DMA((2 * groups,)),
        ],
        compiler_params=params(VMEM),
        cost_estimate=cost(11),
        name="mlp_both",
    )(x, ctx, co, cot, vecs, wo, inner, outer)


def attend_back_kernel(
    first, place_ref, len_ref, near_ref, far_ref, kv_ref, q_ref, lse_ref, ctx_ref, dctx_ref,
    dqc_ref, base_ref, gbefore_ref, gafter_ref, wk_ref, wv_ref, wq_ref,
    pnear_ref, pfar_ref, dq_ref, own_ref, gkv_ref, dkv_ref, acc_ref,
):
    chunks, _, local, width = near_ref.shape
    half = width // 2
    pairs = half // 128
    length = len_ref[first + pl.program_id(0)]
    acc_ref[...] = jnp.zeros_like(acc_ref)

    @pl.when(pl.program_id(0) == 0)
    def _():
        gkv_ref[...] = jnp.zeros_like(gkv_ref)

    rows_q, rows_d, weighted = [], [], []
    unit = jnp.ones((8, 128), BF)
    for p in range(pairs):
        lanes = slice(p * 128, (p + 1) * 128)
        rows_q.append(stacked(q_ref[0, :, lanes]) * BF(SCALE))
        dctx = dctx_ref[0, :, lanes]
        rows_d.append(stacked(dctx))
        product = stacked(dctx.astype(F32) * ctx_ref[0, :, lanes])
        big = product.astype(BF)
        rest = (product - big.astype(F32)).astype(BF)
        weighted.append((dot_nt(unit, big) + dot_nt(unit, rest))[0:1])

    @pl.loop(0, chunks)
    def _(i):
        low, high, start = chunk_rows(place_ref, i, local)

        @pl.when(start < length)
        def _():
            valid = valid_rows(low, high, local, length)
            for p in range(pairs):
                lanes = slice(p * 128, (p + 1) * 128)
                vlanes = slice(half + p * 128, half + (p + 1) * 128)
                keys = kv_ref[0, i, :, lanes]
                scores = jnp.where(valid, dot_nt(keys, rows_q[p]), NEGATIVE)
                probs = jnp.exp(scores - lse_ref[0, p : p + 1, :])
                dprobs = dot_nt(kv_ref[0, i, :, vlanes], rows_d[p])
                dscores = (probs * (dprobs - weighted[p])).astype(BF)
                dkv_ref[:, lanes] = dot(dscores, rows_q[p]).astype(BF)
                dkv_ref[:, vlanes] = dot(probs.astype(BF), rows_d[p]).astype(BF)
                acc_ref[p] += dot_tn(keys, dscores)
            dkv = dkv_ref[...]
            x = jnp.concatenate([near_ref[i, 0], far_ref[i, 0]], axis=0)
            gkv_ref[...] += dot_tn(x, dkv)
            part = (dot_nt(dkv[:, :half], wk_ref[...]) + dot_nt(dkv[:, half:], wv_ref[...])).astype(BF)
            pnear_ref[i, 0] = part[:local]
            pfar_ref[i, 0] = part[local:]

        @pl.when(start >= length)
        def _():
            pnear_ref[i, 0] = jnp.zeros((local, width), BF)
            pfar_ref[i, 0] = jnp.zeros((local, width), BF)

    for p in range(pairs):
        lanes = slice(p * 128, (p + 1) * 128)
        dq_ref[0, :, lanes] = (unstacked(acc_ref[p]) * SCALE + dqc_ref[0, :, lanes]).astype(BF)
    own_ref[0] = base_ref[0] + dot_nt(dq_ref[0], wq_ref[...])

    me = place_ref[0]
    for r in range(2 * chunks):
        target = pnear_ref if r < chunks else pfar_ref

        @pl.when(place_ref[r] == me - 1)
        def _():
            edge = target[r % chunks, 0, local - 2 * PAD :, :].astype(F32)
            edge = jnp.concatenate([edge[:PAD], edge[PAD:] + gbefore_ref[0]], axis=0)
            target[r % chunks, 0, local - 2 * PAD :, :] = edge.astype(BF)

        @pl.when(place_ref[r] == me + 1)
        def _():
            edge = target[r % chunks, 0, : 2 * PAD, :].astype(F32)
            edge = jnp.concatenate([edge[:PAD] + gafter_ref[0], edge[PAD:]], axis=0)
            target[r % chunks, 0, : 2 * PAD, :] = edge.astype(BF)


def run_attend_back(place, lengths, first, near, far, kv, q, lse, ctx, dctx, conv, wk, wv, wq):
    chunks, _, local, width = near.shape
    half, seqs = width // 2, GROUP
    pairs = half // 128
    block = pl.BlockSpec((chunks, 1, local, width), lambda s, *_: (0, s, 0, 0))
    out_block = pl.BlockSpec((chunks, 1, local, width), lambda s, *_: (0, s, 0, 0))
    parts = shaped((chunks, seqs, local, width), BF, True)
    return pl.pallas_call(
        functools.partial(attend_back_kernel, first),
        out_shape=[
            parts, parts, jax.ShapeDtypeStruct((seqs, local, half), BF),
            jax.ShapeDtypeStruct((seqs, local, width), F32), shaped((width, width), F32, True),
        ],
        grid_spec=pltpu.PrefetchScalarGridSpec(
            num_scalar_prefetch=2,
            grid=(seqs,),
            in_specs=[
                block, block, per_seq(*kv.shape[1:]), pl.BlockSpec((1, local, half), lambda s, *_: (s + first, 0, 0)),
                per_seq(*lse.shape[1:]), per_seq(local, half), per_seq(local, half),
                *(per_seq(*c.shape[1:]) for c in conv), *(whole(w.shape) for w in (wk, wv, wq)),
            ],
            out_specs=[out_block, out_block, per_seq(local, half), per_seq(local, width), whole((width, width))],
            scratch_shapes=[pltpu.VMEM((2 * local, width), BF), pltpu.VMEM((pairs, 128, 2 * local), F32)],
        ),
        compiler_params=params(VMEM),
        cost_estimate=cost(16),
        name="attn_bwd",
    )(place, lengths, in_hbm(near), in_hbm(far), in_hbm(kv), q, lse, ctx, dctx, *conv, wk, wv, wq)


def conv_backward_kernel(
    edge_ref, before_ref, x_ref, after_ref, q_ref, ka_ref, kern_ref, cve_ref, dco_ref, dhs_ref,
    wc_ref, dep_ref, wp_ref, kw_ref, ones_ref, sel_ref,
    dqc_ref, base_ref, gbefore_ref, gafter_ref, dcve_ref, xe_ref, dka_ref, dlog_ref, gdep_ref,
    xes_ref, dxe_ref, dce_ref,
):
    local, half = x_ref.shape[1], wc_ref.shape[1]
    ext = local + 2 * PAD
    queries = q_ref[0].astype(F32)
    dco = dco_ref[0]
    dce_ref[...] = jnp.zeros_like(dce_ref)
    dkerns = []
    shared = jnp.zeros((local, half), F32)
    for j in range(KERNEL):
        rows = slice(PAD - REACH + j, PAD - REACH + j + local)
        kern = kern_ref[0, :, j * half : (j + 1) * half]
        dce_ref[rows, :] += kern * dco
        product = dco * cve_ref[0, rows, :]
        high = product.astype(BF)
        rest = (product - high.astype(F32)).astype(BF)
        dkern = dot(high, ones_ref[...]) + dot(rest, ones_ref[...])
        shared += kern * dkern
        dkerns.append(dkern)
    compact = jnp.zeros((local, 128), F32)
    for j in range(KERNEL):
        kern = kern_ref[0, :, j * half : (j + 1) * half]
        compact += dot((kern * (dkerns[j] - shared)).astype(BF), sel_ref[j])
    dlog = compact.astype(BF)
    dlog_ref[0] = dlog
    dca = dot_nt(dlog, kw_ref[...])
    dka = (dca * queries).astype(BF)
    dka_ref[0] = dka
    dqc_ref[0] = dca * ka_ref[0]
    fill_extended(before_ref, x_ref, after_ref, xes_ref)
    xe_ref[0] = xes_ref[...].astype(BF)
    ddw = dot_nt(dka, wp_ref[...])
    dxe_ref[...] = jnp.zeros_like(dxe_ref)
    taps = []
    for j in range(KERNEL):
        rows = slice(PAD - REACH + j, PAD - REACH + j + local)
        taps.append(jnp.sum(ddw * xes_ref[rows, :], axis=0, keepdims=True))
        dxe_ref[rows, :] += ddw * dep_ref[j : j + 1, :]
    taps.append(jnp.zeros((16 - KERNEL, x_ref.shape[2]), F32))
    gdep_ref[0] = jnp.concatenate(taps, axis=0)
    row = lax.broadcasted_iota(jnp.int32, (ext, 1), 0)
    inside = (row >= edge_ref[0]) & (row < edge_ref[1])
    dcve = jnp.where(inside, dce_ref[...], 0.0).astype(BF)
    dcve_ref[0] = dcve
    dxe_ref[...] += dot_nt(dcve, wc_ref[...])
    base_ref[0] = dhs_ref[0] + dxe_ref[PAD : PAD + local, :]
    gbefore_ref[0] = dxe_ref[0:PAD, :]
    gafter_ref[0] = dxe_ref[PAD + local :, :]


def run_conv_backward(edges, g, before, x, after, saved, grads, weights):
    _, local, width = x.shape
    seqs, half, ext = GROUP, width // 2, local + 2 * PAD
    outs = [
        ((local, half), F32), ((local, width), F32), ((PAD, width), F32), ((PAD, width), F32), ((ext, half), BF),
        ((ext, width), BF), ((local, half), BF), ((local, 128), BF), ((16, width), F32),
    ]
    part = lambda a: pl.BlockSpec((1,) + a.shape[1:], lambda s, *_: (s + g * seqs, 0, 0))
    return pl.pallas_call(
        conv_backward_kernel,
        out_shape=[jax.ShapeDtypeStruct((seqs,) + s, d) for s, d in outs],
        grid_spec=pltpu.PrefetchScalarGridSpec(
            num_scalar_prefetch=1,
            grid=(seqs,),
            in_specs=[part(a) for a in (before, x, after, *saved)]
            + [per_seq(*a.shape[1:]) for a in grads]
            + [whole(w.shape) for w in weights],
            out_specs=[per_seq(*s) for s, _ in outs],
            scratch_shapes=[pltpu.VMEM((ext, width), F32), pltpu.VMEM((ext, width), F32), pltpu.VMEM((ext, half), F32)],
        ),
        compiler_params=params(VMEM),
        cost_estimate=cost(9),
        name="conv_bwd",
    )(edges, before, x, after, *(in_hbm(a) if a.shape[-1] > width else a for a in saved), *grads, *weights)


def square_piece(acc_ref, lead, seq, dp, rows_each):
    half = acc_ref.shape[-1] // 2
    row = pl.multiple_of(seq * rows_each + (dp % 2) * UNIT, 16)
    lane = pl.multiple_of((dp // 2) * half, 128)
    return acc_ref[lead + (pl.ds(row, UNIT), pl.ds(lane, half))]


def spread(place_ref, dplace_ref, near_ref, far_ref, rows, read):
    dps, chunks = near_ref.shape[:2]
    for r in range(2 * chunks):
        target = near_ref if r < chunks else far_ref

        @pl.loop(0, dps)
        def _(j):
            target[j, r % chunks, rows] = read(place_ref[r], dplace_ref[j]).astype(BF)


def sum_tn(lefts, rights):
    return functools.reduce(jnp.add, [dot_tn(a[...], b[...]) for a, b in zip(lefts, rights)])


def early_kernel(count, place_ref, dplace_ref, *refs):
    acts, douts, h1bs, dpres, ctxs, cos, dprojs = (refs[i * count : (i + 1) * count] for i in range(7))
    near_ref, far_ref, outer_ref, inner_ref, square_ref = refs[7 * count :]
    u = pl.program_id(0)
    half = near_ref.shape[3]
    n = place_ref.shape[0]
    put = functools.partial(spread, place_ref, dplace_ref, near_ref, far_ref, slice(0, UNIT))

    @pl.when(u < 2)
    def _():
        outer_ref[...] = sum_tn(acts, douts)
        each = outer_ref.shape[0] // n
        put(lambda s, d: outer_ref[pl.ds(pl.multiple_of(s * each + d * UNIT, 16), UNIT), :])

    @pl.when((u >= 2) & (u < 4))
    def _():
        inner_ref[...] = sum_tn(h1bs, dpres)
        put(
            lambda s, d: inner_ref[
                pl.ds(pl.multiple_of(s * UNIT, 16), UNIT), pl.ds(pl.multiple_of(d * half, 128), half)
            ]
        )

    @pl.when(u == 4)
    def _():
        square_ref[:half] = sum_tn(ctxs, dprojs)
        square_ref[half:] = sum_tn(cos, dprojs)
        put(lambda s, d: square_piece(square_ref, (), s, d, square_ref.shape[0] // n))


def run_early(place, dplace, acts, douts, h1bs, dpres, ctxs, co, dprojs):
    count = len(acts)
    n, dps = place.shape[0], dplace.shape[0]
    rows, ff = acts[0].shape
    width = douts[0].shape[1]
    half = width // 2
    first = lambda u: jnp.minimum(u, 1)
    second = lambda u: jnp.clip(u - 2, 0, 1)
    spec = lambda lanes, f: pl.BlockSpec((rows, lanes), lambda u, *_: (0, f(u)))
    fixed = lambda a: pl.BlockSpec(a.shape, lambda u, *_: (0, 0), pipeline_mode=pl.Buffered(1))
    third = lambda lanes: [
        pl.BlockSpec((rows, lanes), lambda u, *_, g=g: (g, 0), pipeline_mode=pl.Buffered(1)) for g in range(count)
    ]
    ins = (
        [spec(ff // 2, first)] * count + [spec(half, first)] * count + [spec(half, second)] * count
        + [spec(ff // 2, second)] * count + [fixed(c) for c in ctxs] + third(half) + [fixed(a) for a in dprojs]
    )
    out = pl.BlockSpec((dps, n // 2, UNIT, half), lambda u, *_: (0, 0, u, 0))
    shape = jax.ShapeDtypeStruct((dps, n // 2, 5 * UNIT, half), BF)
    return pl.pallas_call(
        functools.partial(early_kernel, count),
        out_shape=[shape, shape],
        grid_spec=pltpu.PrefetchScalarGridSpec(
            num_scalar_prefetch=2,
            grid=(5,),
            in_specs=ins,
            out_specs=[out, out],
            scratch_shapes=[
                pltpu.VMEM((ff // 2, half), F32), pltpu.VMEM((half, ff // 2), F32), pltpu.VMEM((width, width), F32)
            ],
        ),
        compiler_params=params(VMEM),
        cost_estimate=cost(15),
        name="wgrad_early",
    )(place, dplace, *acts, *douts, *h1bs, *dpres, *ctxs, *([co] * count), *dprojs)


LATE_ROWS = 144


def late_kernel(count, place_ref, dplace_ref, x_ref, dw_ref, ca_ref, *refs):
    gkvs, dqs, dlogs, xes, dcves, dkas = (refs[i * count : (i + 1) * count] for i in range(6))
    small_ref, near_ref, far_ref, kv_ref, cp_ref, q_ref, kn_ref = refs[6 * count :]
    half = near_ref.shape[3]
    n = place_ref.shape[0]
    rows = dqs[0].shape[0]
    kv_ref[...] = functools.reduce(jnp.add, [g[...] for g in gkvs])
    cut = lambda left: [left[g * rows : (g + 1) * rows, :] for g in range(count)]
    cp_ref[:, :half] = sum_tn(xes, dcves)
    cp_ref[:, half:] = sum_tn(cut(dw_ref), dkas)
    q_ref[...] = sum_tn(cut(x_ref), dqs)
    kn_ref[...] = sum_tn(cut(ca_ref), dlogs)
    each = kv_ref.shape[0] // n
    piece = each // QUARTERS

    def rest(s, d):
        query = q_ref[pl.ds(pl.multiple_of(s * each + d * piece, 8), piece), :]
        kernel = kn_ref[pl.ds(pl.multiple_of(s * (half // n), 16), half // n), :]
        kernel = jnp.concatenate([kernel[i * 16 : (i + 1) * 16] for i in range(3)], axis=1)
        small = jnp.concatenate([small_ref[s], jnp.zeros((16, half - small_ref.shape[2]), F32)], axis=1)
        other = jnp.where(d == 0, kernel, jnp.where(d == 1, small, 0.0))
        return jnp.concatenate([query, other, jnp.zeros((LATE_ROWS - 2 * UNIT - 16 - piece, half), F32)], axis=0)

    put = functools.partial(spread, place_ref, dplace_ref, near_ref, far_ref)
    put(slice(0, UNIT), lambda s, d: square_piece(kv_ref, (), s, d, each))
    put(slice(UNIT, 2 * UNIT), lambda s, d: square_piece(cp_ref, (), s, d, each))
    put(slice(2 * UNIT, LATE_ROWS), rest)


def run_late(place, dplace, x, dw, ca, gkvs, dqs, dlogs, xes, dcves, dkas, small):
    count = len(gkvs)
    n, dps = place.shape[0], dplace.shape[0]
    width = x.shape[1]
    half = width // 2
    args = (x, dw, ca, *gkvs, *dqs, *dlogs, *xes, *dcves, *dkas, small)
    shape = (dps, n // 2, LATE_ROWS, half)
    return pl.pallas_call(
        functools.partial(late_kernel, count),
        out_shape=[jax.ShapeDtypeStruct(shape, BF)] * 2,
        grid_spec=pltpu.PrefetchScalarGridSpec(
            num_scalar_prefetch=2,
            grid=(1,),
            in_specs=[whole(a.shape) for a in args],
            out_specs=[whole(shape)] * 2,
            scratch_shapes=[
                pltpu.VMEM((width, width), F32), pltpu.VMEM((width, width), F32), pltpu.VMEM((width, half), F32),
                pltpu.VMEM((half, 128), F32),
            ],
        ),
        compiler_params=params(VMEM),
        cost_estimate=cost(6),
        name="wgrad_late",
    )(place, dplace, *args)


def peers(value, axis, step):
    count = lax.axis_size(axis)
    return lax.ppermute(value, axis, [(i, i ^ step) for i in range(count)])


def bits_of(count):
    return [1 << b for b in reversed(range(count.bit_length() - 1))]


def after(value, *others):
    return lax.optimization_barrier((value, *others))[0] if others else value


def xor_step(slot):
    return sum(bit for k, bit in enumerate(bits_of(lax.axis_size("seq"))) if slot >> k & 1)


def gather_direct(x):
    n_seq = lax.axis_size("seq")
    come = [peers(x[None], "seq", xor_step(i)) for i in range(1, n_seq // 2)]
    covers = yield x, come[0]
    near = jnp.concatenate([x[None], *(after(c, *covers) for c in come)], axis=0)
    come = peers(near, "seq", 1)
    yield near, come
    yield near, come


def gather_steps(x):
    bits = bits_of(lax.axis_size("seq"))
    near = x[None]
    for bit in bits[:-1]:
        come = peers(near, "seq", bit)
        covers = yield near, come
        near = jnp.concatenate([near, after(come, *covers)], axis=0)
    come = peers(near, "seq", bits[-1])
    yield near, come
    yield near, come


def scatter_steps(near, far):
    bits = bits_of(lax.axis_size("seq"))
    come = peers(far, "seq", bits[-1])
    covers = yield far, come
    parts = [near, after(come, *covers)]
    left = near.shape[0]
    for bit in reversed(bits[:-1]):
        left //= 2
        sent = functools.reduce(jnp.add, [p[left : 2 * left].astype(F32) for p in parts]).astype(BF)
        come = peers(sent, "seq", bit)
        covers = yield sent, come
        parts.append(after(come, *covers))
    yield functools.reduce(jnp.add, [p[0].astype(F32) for p in parts])


def reduce_steps(near, far):
    n_seq, n_dp = lax.axis_size("seq"), lax.axis_size("dp")
    quarters = near.shape[0]
    come = peers(far, "seq", 1)
    covers = yield far, come
    come = after(come, *covers)
    pieces = [near[j].astype(F32) + come[j].astype(F32) for j in range(quarters)]
    sent = [p.astype(BF) for p in pieces[1:]]
    moved = [peers(p, "dp", j + 1) for j, p in enumerate(sent[:-1])]
    covers = yield sent[0], moved[0]
    moved = [after(m, *covers) for m in moved]
    moved.append(peers(after(sent[-1], *covers), "dp", quarters - 1))
    covers = yield sent[-1], moved[-1]
    moved[-1] = after(moved[-1], *covers)
    total = functools.reduce(jnp.add, [m.astype(F32) for m in moved], pieces[0])
    sent = [total[i].astype(BF) for i in range(1, n_seq // 2)]
    moved = [peers(p, "seq", xor_step(i + 1)) for i, p in enumerate(sent)]
    covers = yield sent[-1], moved[-1]
    mine = functools.reduce(jnp.add, [after(m, *covers).astype(F32) for m in moved], total[0]).astype(BF)
    step = quarters
    while step < n_dp:
        mine = (mine.astype(F32) + peers(mine, "dp", step).astype(F32)).astype(BF)
        step *= 2
    yield jnp.stack([mine] + [peers(mine, "dp", j) for j in range(1, quarters)])


def covered(steps, *kernels):
    return steps.send(kernels)


def finish(steps):
    value = None
    while True:
        try:
            value = steps.send(())
        except StopIteration:
            return value


def in_order(quarters):
    dp = lax.axis_index("dp") % quarters.shape[0]
    return [
        lax.dynamic_index_in_dim(quarters, dp ^ q, 0, keepdims=False).astype(F32) for q in range(quarters.shape[0])
    ]


def from_square(parts):
    return jnp.concatenate(
        [jnp.concatenate([parts[0], parts[1]], axis=0), jnp.concatenate([parts[2], parts[3]], axis=0)], axis=1
    )


def body(
    hidden, lengths, cotangent, query_weight, key_weight, value_weight, depth_weight, point_weight, kernel_weight,
    convval_weight, output_weight, norm_gain, norm_bias, inner_weight, outer_weight, final_gain, final_bias,
):
    seqs, local, width = hidden.shape
    half = width // 2
    n_seq = lax.axis_size("seq")
    my, dp = lax.axis_index("seq").astype(jnp.int32), lax.axis_index("dp").astype(jnp.int32)
    groups = seqs // GROUP
    bits = bits_of(n_seq)
    shift = [sum(bit for k, bit in enumerate(bits) if r >> k & 1) for r in range(n_seq)]
    place = my ^ jnp.array(shift, jnp.int32)
    dplace = dp % QUARTERS ^ jnp.arange(QUARTERS, dtype=jnp.int32)
    ends = n_seq - 1
    ahead, behind = [(i, i + 1) for i in range(ends)], [(i + 1, i) for i in range(ends)]
    before = lax.ppermute(hidden[:, local - PAD :], "seq", ahead)
    after_rows = lax.ppermute(hidden[:, :PAD], "seq", behind)

    gathers = [gather_direct(after(hidden[:GROUP], before, after_rows))]
    next(gathers[0])

    dep = jnp.pad(depth_weight.astype(F32), ((0, 16 - KERNEL), (0, 0)))
    by_tap = kernel_weight.reshape(half, HEADS, KERNEL).swapaxes(1, 2)
    wke = jnp.repeat(by_tap, HEAD_SIZE, axis=2).reshape(half, KERNEL * half)
    kw = jnp.pad(kernel_weight, ((0, 0), (0, 128 - HEADS * KERNEL)))
    lane = jnp.arange(half)
    ones = (lane[:, None] // HEAD_SIZE == lane[None, :] // HEAD_SIZE).astype(BF)
    column = jnp.where(lane % HEAD_SIZE == 0, lane // HEAD_SIZE * KERNEL, -128)
    sel = (column[None, :, None] + jnp.arange(KERNEL)[:, None, None] == jnp.arange(128)[None, None, :]).astype(BF)
    vecs = jnp.stack([norm_gain, norm_bias, final_gain, final_bias] * 2)
    edges = jnp.stack([jnp.where(my > 0, 0, PAD), jnp.where(my < ends, local + 2 * PAD, local + PAD)])

    q, ka, ca, dw, kern, co, cve = run_conv_forward(
        before, hidden, after_rows, query_weight, convval_weight, dep, point_weight, wke
    )
    flat = lambda a: a.reshape(-1, a.shape[-1])
    x_rows, cot_rows, co_rows = flat(hidden), flat(cotangent), flat(co)

    split = lambda a: a.reshape(GROUP, local, -1)
    full = []
    ctxs, mlps, convs, backs, attends = [], [], [], [], []

    def attend(g, *gates):
        near, far = full[g]
        attends.append(
            run_attend(place, after(lengths, *gates), g * GROUP, near, far, q, key_weight, value_weight)
        )
        ctxs.append(flat(attends[g][3]))

    def mlp(g, *gates):
        mlps.append(
            run_mlp(
                g, x_rows, after(ctxs[g], *gates), co_rows, cot_rows, output_weight, inner_weight, outer_weight, vecs
            )
        )

    def conv(g, *gates):
        convs.append(
            run_conv_backward(
                after(edges, *gates), g, before, hidden, after_rows, (q, ka, kern, cve),
                (split(mlps[g][3]), split(mlps[g][1])),
                (convval_weight, dep, point_weight, kw, ones, sel),
            )
        )

    def back(g, *gates):
        near, far = full[g]
        kv, lse, ctx, _ = attends[g]
        backs.append(
            run_attend_back(
                place, after(lengths, *gates), g * GROUP, near, far, kv, q, lse, ctx, split(mlps[g][2]),
                convs[g][:4], key_weight, value_weight, query_weight,
            )
        )
        return scatter_steps(*backs[g][:2])

    covered(gathers[0], q, kw, ones, sel, vecs)
    full.append(finish(gathers[0]))
    gathers.append(gather_steps(after(hidden[GROUP : 2 * GROUP], full[0][0])))
    next(gathers[1])
    attend(0)
    sent, _ = covered(gathers[1], ctxs[0])
    gathers.append(gather_steps(after(hidden[2 * GROUP :], sent)))
    next(gathers[2])
    mlp(0, sent)
    conv(0)
    sent, _ = covered(gathers[1], convs[0][8])
    sent2, _ = covered(gathers[2], convs[0][8])
    scatters = [back(0, sent, sent2)]
    next(scatters[0])
    full.append(finish(gathers[1]))
    sent2, _ = covered(gathers[2], backs[0][2])
    attend(1, backs[0][2], sent2)
    sent, _ = covered(scatters[0], ctxs[1])
    full.append(finish(gathers[2]))
    mlp(1, sent)
    attend(2, mlps[1][7])
    sent, _ = covered(scatters[0], ctxs[2])
    mlp(2, sent)
    early = run_early(
        place, dplace, *([m[i] for m in mlps] for i in (8, 5, 4, 9)), ctxs, co_rows, [m[6] for m in mlps]
    )
    early_steps = reduce_steps(*early)
    next(early_steps)
    conv(1, early[0])
    sent, _ = covered(early_steps, convs[1][8])
    scatters.append(back(1, sent))
    next(scatters[1])
    covered(early_steps, backs[1][2])
    conv(2, backs[1][2])
    sent, _ = covered(scatters[1], convs[2][8])
    scatters.append(back(2, sent))
    next(scatters[2])
    pick = lambda parts, i: [flat(p[i]) for p in parts]
    sums = functools.reduce(jnp.add, [m[7] for m in mlps])[:4]
    gdep = functools.reduce(jnp.add, [c[8][s] for c in convs for s in range(GROUP)])[:KERNEL]
    small = jnp.concatenate([gdep, sums, jnp.zeros((16 - KERNEL - 4, width), F32)], axis=0)
    small = small.reshape(16, n_seq, width // n_seq).swapaxes(0, 1)
    late = run_late(
        place, dplace, x_rows, flat(dw), flat(ca), [b[4] for b in backs], pick(backs, 2), pick(convs, 7),
        pick(convs, 5), pick(convs, 4), pick(convs, 6), small,
    )
    late_steps = reduce_steps(*late)
    next(late_steps)
    sent, _ = covered(scatters[1], backs[2][2])
    sent2, _ = covered(early_steps, backs[2][2])
    sent, _ = covered(scatters[2], late[0])
    covered(late_steps, sent)
    covered(late_steps)
    early = covered(early_steps, late[0])
    covered(scatters[2])
    covered(late_steps)
    late = finish(late_steps)
    grad_input = jnp.concatenate([b[3] + finish(p) for b, p in zip(backs, scatters)], axis=0)
    output = jnp.concatenate([m[0] for m in mlps], axis=0).reshape(seqs, local, width)

    early, late = in_order(early), in_order(late)
    unit = lambda parts, u: [p[u * UNIT : (u + 1) * UNIT] for p in parts]
    r_outer = jnp.stack([jnp.concatenate(unit(early, u), axis=0) for u in range(2)])
    r_inner = jnp.stack([jnp.concatenate(unit(early, u), axis=1) for u in (2, 3)])
    r_output = from_square(unit(early, 4))
    r_kv, r_cp = from_square(unit(late, 0)), from_square(unit(late, 1))
    rest = [p[2 * UNIT :] for p in late]
    each = width // n_seq
    piece = each // QUARTERS
    r_query = jnp.concatenate([m[:piece] for m in rest], axis=0)
    r_kernel = jnp.concatenate(
        [rest[0][piece : piece + 16, i * 128 : i * 128 + HEADS * KERNEL] for i in range(3)], axis=0
    )
    r_small = rest[1][piece : piece + 16, :each]
    r_depth = r_small[:KERNEL]
    r_ngain, r_nbias, r_fgain, r_fbias = (r_small[KERNEL + i] for i in range(4))
    return (
        output, grad_input.astype(BF), r_query, r_kv[:, :half], r_kv[:, half:], r_depth, r_cp[:, half:], r_kernel,
        r_cp[:, :half], r_output, r_ngain, r_nbias, r_inner, r_outer, r_fgain, r_fbias,
    )


def solution(mesh):
    rows = P("dp", "seq", None)
    return jax.shard_map(
        body,
        mesh=mesh,
        in_specs=(rows, P("dp"), rows) + (P(),) * 14,
        out_specs=(rows, rows)
        + (P("seq", None),) * 3
        + (P(None, "seq"),)
        + (P("seq", None),) * 4
        + (P("seq"),) * 2
        + (P(None, "seq", None),) * 2
        + (P("seq"),) * 2,
        check_vma=False,
    )
```
